512 devices in a mesh: takers: 64 (over z, x), nodes: 8 (over y, core).
Axes of the slice: x: 4, y: 4, z: 16, core: 2. Of those that a mesh axis runs over, the one named last changes fastest.
Arguments:
- slopes: bfloat16 [3, 65536], P(None, 'takers'), may hold values from 0.29882812 to 1.5
- intercepts: bfloat16 [65536], P('takers'), may hold values from -3 to 3
- guessing: bfloat16 [65536], P('takers'), may hold values from 0.049804688 to 0.29882812
- responses: int32 [256, 12, 128, 128], P('takers'), may hold values from 0 to 2, as said below
- tile_items: int32 [256, 12], P('takers'), may hold values from 0 to 511, as said below
- tile_count: int32 [256], P('takers'), may hold values from 4 to 12, as said below
Outputs:
- new_params: float32 [4, 65536], P(None, 'takers')
- marginal: float32 [32768], P('takers')
- posterior_mean: float32 [3, 32768], P(None, 'takers')
The draws below stay inside these ranges and needn't reach their ends.
Inputs may be any that keep to these rules, and one draw needn't show every extreme that they name: `tile_items`: within a row block the used slots name distinct item blocks; some row block uses all 12 slots. `tile_count`: some row block uses all 12 slots; slots at or beyond the count are ignored. `responses`: 0 means not answered, 1 a wrong answer, 2 a right answer; most entries are 0.
All inputs are finite; a program needn't handle non-finite values.
Results may differ from the reference program's by a relative error of at most 0.0041.
Values may be sent and summed in bfloat16 or wider, within the bound.
No kernel may reach another device: no remote copies, remote signals or barrier semaphores. Data moves between devices by JAX's collectives and lax.ppermute only.
A program may use at most 64 MiB of HBM per device.

```python
import math
import jax
import jax.numpy as jnp
from jax import lax

ITEMS = 65536
TILE = 128
NODES_1D = 16
KT = 12
NODES = 4096
TAKERS = 32768
ROWBLK = 256
BLOCKS = 512


def draw_tile_items(key, part):
    row_keys = jax.random.split(jax.random.fold_in(key, 11), ROWBLK)
    return jax.vmap(lambda row_key: jax.random.permutation(row_key, ITEMS // TILE)[:KT])(row_keys).astype(jnp.int32)


def draw_tile_count(key, part):
    counts = jax.random.randint(jax.random.fold_in(key, 23), (ROWBLK,), max(1, KT // 3), KT + 1, dtype=jnp.int32)
    full_row = jax.random.randint(jax.random.fold_in(key, 29), (), 0, ROWBLK, dtype=jnp.int32)
    return counts.at[full_row].set(KT)


def draw_responses(key, part):
    shape = (ROWBLK, KT, TILE, TILE)
    seen = jax.random.randint(jax.random.fold_in(key, 31), shape, 0, 8, dtype=jnp.int32) == 0
    dense_taker = jax.random.randint(jax.random.fold_in(key, 41), (ROWBLK, 1, TILE, 1), 0, 16, dtype=jnp.int32) == 0
    seen = jnp.logical_or(seen, dense_taker)
    right_bit = jax.random.randint(jax.random.fold_in(key, 37), shape, 0, 2, dtype=jnp.int32)
    codes = jnp.where(seen, 1 + right_bit, 0).astype(jnp.int32)
    return codes.at[0, 0, 0, 0].set(2).at[0, 0, 0, 1].set(1)


def steps_of(key, extent, shards, low, largest):
    factor_of = 1.0
    for position, shards_of in shards:
        draws = jax.random.uniform(jax.random.fold_in(jax.random.fold_in(key, 6), position), (shards_of,), jnp.float32, low / len(shards), largest / len(shards))
        factor_of = factor_of * jnp.repeat(jnp.exp(draws), extent[position] // shards_of).reshape((-1,) + (1,) * (len(extent) - 1 - position))
    return factor_of


def scatter_about(own_key, extent, width, most, pieces=(), kind=jnp.bfloat16):
    loudness = steps_of(own_key, extent, pieces, -0.22, 0.18) if pieces else 1.0
    values = jax.random.normal(own_key, extent, jnp.float32) * width * loudness
    return jnp.minimum(jnp.maximum(values, -most), most).astype(kind)


def setup_inputs(seed: int = 0) -> dict:
    keys = jax.random.split(jax.random.key(seed), 7)
    slopes = jnp.clip(jnp.exp(math.log(1.5) - 1.6133518 * jax.random.uniform(keys[0], (3, ITEMS), jnp.float32) ** steps_of(keys[0], (3, ITEMS), ((1, 64),), -0.2, 0.2)), 0.29882812, 1.5).astype(jnp.bfloat16)
    intercepts = scatter_about(keys[1], (ITEMS,), 1.0, 3.0, ((0, 64),))
    guessing = jnp.clip(0.049804688 + 0.24902344 * jax.random.uniform(keys[2], (ITEMS,), jnp.float32) ** steps_of(keys[2], (ITEMS,), ((0, 64),), -0.2, 0.2), 0.049804688, 0.29882812).astype(jnp.bfloat16)
    responses = draw_responses(jax.random.fold_in(keys[6], 71), 0)
    tile_items = draw_tile_items(jax.random.fold_in(keys[6], 71), 0)
    tile_count = draw_tile_count(jax.random.fold_in(keys[6], 71), 0)
    return dict(slopes=slopes, intercepts=intercepts, guessing=guessing, responses=responses, tile_items=tile_items, tile_count=tile_count)


def node_grid(first_node, how_many, grid_side):
    node_index = first_node + jnp.arange(how_many, dtype=jnp.int32)
    lattice = jnp.stack([node_index // (grid_side * grid_side), (node_index // grid_side) % grid_side, node_index % grid_side]).astype(jnp.float32)
    return -3.0 + 6.0 * lattice / (grid_side - 1)


def log_prior(node_points, grid_side):
    whole = node_grid(0, grid_side ** 3, grid_side)
    log_total = jnp.log(jnp.sum(jnp.exp(-0.5 * jnp.sum(whole * whole, axis=0))))
    return -0.5 * jnp.sum(node_points * node_points, axis=0) - log_total


def tile_logits(slope_blk, icpt_blk, node_points):
    return (slope_blk[:, 0, :, None] * node_points[0] + slope_blk[:, 1, :, None] * node_points[1]
            + slope_blk[:, 2, :, None] * node_points[2] + icpt_blk[:, :, None])


def reference(slopes, intercepts, guessing, responses, tile_items, tile_count):
    grid_side = NODES_1D
    node_points = node_grid(0, NODES, grid_side)
    prior_here = log_prior(node_points, grid_side)
    slope_tab = slopes.astype(jnp.float32).reshape(3, BLOCKS, TILE)
    icpt_tab = intercepts.astype(jnp.float32).reshape(BLOCKS, TILE)
    guess_tab = guessing.astype(jnp.float32).reshape(BLOCKS, TILE)
    features = jnp.concatenate([node_points, jnp.ones((1, NODES), jnp.float32)], axis=0)

    def per_block(inputs):
        answers, block_ids, filled = inputs
        live_mask = (jnp.arange(KT, dtype=jnp.int32) < filled).astype(jnp.float32)[:, None, None]
        slope_blk = jnp.transpose(slope_tab[:, block_ids], (1, 0, 2))
        logits = tile_logits(slope_blk, icpt_tab[block_ids], node_points)
        guess_rate = guess_tab[block_ids][:, :, None]
        sig_pos = jax.nn.sigmoid(logits)
        sig_neg = jax.nn.sigmoid(-logits)
        correct = guess_rate + (1.0 - guess_rate) * sig_pos
        log_miss = jnp.log(1.0 - guess_rate) + jax.nn.log_sigmoid(-logits)
        log_right = (jnp.log(correct) * live_mask).astype(jnp.bfloat16)
        log_wrong = (log_miss * live_mask).astype(jnp.bfloat16)
        right_f = (answers == 2).astype(jnp.float32)
        wrong_f = (answers == 1).astype(jnp.float32)
        answered_f = right_f + wrong_f
        loglik = (jnp.einsum('kti,kiq->tq', right_f, log_right.astype(jnp.float32))
                  + jnp.einsum('kti,kiq->tq', wrong_f, log_wrong.astype(jnp.float32)) + prior_here)
        row_max = jnp.max(loglik, axis=1)
        weights = jnp.exp(loglik - row_max[:, None])
        row_mass = jnp.sum(weights, axis=1)
        moment = jnp.einsum('cq,tq->ct', node_points, weights, precision=lax.Precision.HIGHEST)
        log_norm = row_max + jnp.log(row_mass)
        mean_here = moment / row_mass
        posterior = jnp.exp(loglik - log_norm[:, None]).astype(jnp.bfloat16)
        post_f = posterior.astype(jnp.float32)
        correct_mass = jnp.einsum('kti,tq->kiq', right_f, post_f)
        node_mass = jnp.einsum('kti,tq->kiq', answered_f, post_f)
        gradient = (correct_mass - node_mass * correct) * (sig_pos / correct) * live_mask
        fisher = node_mass * (1.0 - guess_rate) * sig_pos * sig_pos * sig_neg / correct * live_mask
        grad_terms = jnp.einsum('kiq,cq->kci', gradient, features, precision=lax.Precision.HIGHEST)
        fisher_terms = jnp.einsum('kiq,cq->kci', fisher, features * features, precision=lax.Precision.HIGHEST)
        return log_norm, mean_here, jnp.concatenate([grad_terms, fisher_terms], axis=1)

    log_norms, means, tile_stats = lax.map(per_block, (responses, tile_items, tile_count))
    marginal = log_norms.reshape(TAKERS)
    posterior_mean = jnp.transpose(means, (1, 0, 2)).reshape(3, TAKERS)
    flat_stats = jnp.transpose(tile_stats, (2, 0, 1, 3)).reshape(8, ROWBLK * KT, TILE)
    item_totals = jnp.zeros((8, BLOCKS, TILE), jnp.float32).at[:, tile_items.reshape(-1)].add(flat_stats)
    item_totals = item_totals.reshape(8, ITEMS)
    current = jnp.concatenate([slopes.astype(jnp.float32), intercepts.astype(jnp.float32)[None]], axis=0)
    new_params = current + item_totals[:4] / (item_totals[4:] + 1.0)
    return new_params, marginal, posterior_mean
```

```python
import functools
import math

import jax
import jax.numpy as jnp
import numpy as np
from jax import lax
from jax.experimental import pallas as pl
from jax.experimental.pallas import tpu as pltpu
from jax.sharding import PartitionSpec as P

SIDE = 16
HALF = SIDE // 2
TILE = 128
KT = 12
SLOTS = 16
F32 = jnp.float32
BF16 = jnp.bfloat16

AXIS = (np.float32(-3.0) + np.float32(6.0) * np.arange(SIDE, dtype=np.float32) / np.float32(15.0)).astype(np.float32)
STEP = 6.0 / 15.0
LOG_TOTAL = 3.0 * math.log(float(np.sum(np.exp(-0.5 * AXIS.astype(np.float64) ** 2))))


def axis_column():
    index = lax.broadcasted_iota(jnp.int32, (SIDE, TILE), 0).astype(F32)
    return -3.0 + 6.0 * index / 15.0


def tile_start(par_ref, k, first):
    a0, a1, a2, d, c = (par_ref[j, pl.ds(k, 1), :] for j in range(5))
    base = jnp.exp(a2 * axis_column() + (a0 * first + a1 * float(AXIS[0]) + d))
    ratio0 = jnp.broadcast_to(jnp.exp(a0 * STEP), (SIDE, TILE))
    ratio1 = jnp.broadcast_to(jnp.exp(a1 * STEP), (SIDE, TILE))
    return base, ratio0, ratio1, c


def likelihood_kernel(sc_ref, got_ref, resp_ref, w_ref, st_ref, par_ref, tab_ref):
    count = sc_ref[1]
    first = -3.0 + STEP * HALF * sc_ref[2].astype(F32)
    par_ref[...] = got_ref[...].astype(F32)
    theta2 = axis_column()
    for j0 in range(HALF):
        theta0 = first + STEP * j0
        for j1 in range(SIDE):
            rows = pl.ds((j0 * SIDE + j1) * SIDE, SIDE)
            w_ref[rows, :] = -0.5 * (theta2 * theta2) - (
                0.5 * (theta0 * theta0) + (0.5 * float(AXIS[j1]) ** 2 + LOG_TOTAL)
            )

    def tile(k, carry):
        codes = jnp.transpose(resp_ref[0, k].astype(F32))
        marks = jnp.concatenate([(codes == 2.0).astype(BF16), (codes == 1.0).astype(BF16)], axis=0)
        base, ratio0, ratio1, c = tile_start(par_ref, k, first)
        c_b = jnp.broadcast_to(c, (SIDE, TILE))
        log_rest = jnp.broadcast_to(jnp.log(1.0 - c), (SIDE, TILE))
        for j0 in range(HALF):
            u = base
            for j1 in range(SIDE):
                rows = pl.ds((j0 * SIDE + j1) * SIDE, SIDE)
                log_one = jnp.log(1.0 + u)
                tab_ref[rows, 0:TILE] = (jnp.log(c_b + u) - log_one).astype(BF16)
                tab_ref[rows, TILE : 2 * TILE] = (log_rest - log_one).astype(BF16)
                u = u * ratio1
            slab = pl.ds(j0 * SIDE * SIDE, SIDE * SIDE)
            w_ref[slab, :] += jnp.dot(tab_ref[slab, :], marks, preferred_element_type=F32)
            base = base * ratio0
        return carry

    lax.fori_loop(0, count, tile, 0)

    top = jnp.full((SIDE, TILE), -jnp.inf, F32)
    for j in range(HALF * SIDE):
        top = jnp.maximum(top, w_ref[pl.ds(j * SIDE, SIDE), :])
    top = jnp.max(top, axis=0, keepdims=True)
    total = jnp.zeros((SIDE, TILE), F32)
    mom0 = jnp.zeros((SIDE, TILE), F32)
    mom1 = jnp.zeros((SIDE, TILE), F32)
    for j0 in range(HALF):
        slab_sum = jnp.zeros((SIDE, TILE), F32)
        for j1 in range(SIDE):
            rows = pl.ds((j0 * SIDE + j1) * SIDE, SIDE)
            w = jnp.exp(w_ref[rows, :] - top)
            w_ref[rows, :] = w
            slab_sum = slab_sum + w
            mom1 = mom1 + float(AXIS[j1]) * w
        total = total + slab_sum
        mom0 = mom0 + (first + STEP * j0) * slab_sum
    mom2 = total * theta2
    st_ref[0:1, :] = top
    for j, part in enumerate((total, mom0, mom1, mom2)):
        st_ref[j + 1 : j + 2, :] = jnp.sum(part, axis=0, keepdims=True)
    st_ref[5:8, :] = jnp.zeros((3, TILE), F32)


def statistics_kernel(sc_ref, got_ref, resp_ref, w_ref, mine_ref, other_ref, out_ref, par_ref, post_ref):
    count = sc_ref[1]
    first = -3.0 + STEP * HALF * sc_ref[2].astype(F32)
    par_ref[...] = got_ref[...].astype(F32)
    mine, other = mine_ref[...], other_ref[...]
    top = jnp.maximum(mine[0:1], other[0:1])
    both = mine[1:5] * jnp.exp(mine[0:1] - top) + other[1:5] * jnp.exp(other[0:1] - top)
    log_norm = top + jnp.log(both[0:1])
    means = both[1:4] / both[0:1]
    scale = jnp.exp(mine[0:1] - log_norm)
    post_ref[...] = (w_ref[...] * scale).astype(BF16)
    out_ref[...] = jnp.zeros(out_ref.shape, F32)
    for j in range(8):
        out_ref[j, KT : KT + 1, :] = log_norm
        out_ref[j, KT + 1 : KT + 4, :] = means
    theta2 = axis_column()

    def tile(k, carry):
        codes = resp_ref[0, k]
        marks = jnp.concatenate([(codes == 2).astype(BF16), (codes > 0).astype(BF16)], axis=1)
        base, ratio0, ratio1, c = tile_start(par_ref, k, first)
        c_b = jnp.broadcast_to(c, (SIDE, TILE))
        zero = jnp.zeros((SIDE, TILE), F32)
        g_all, f_all, g_0, f_0, g_1, f_1 = (zero,) * 6
        for j0 in range(HALF):
            slab = pl.ds(j0 * SIDE * SIDE, SIDE * SIDE)
            counts = jnp.dot(post_ref[slab, :], marks, preferred_element_type=F32)
            theta0 = first + STEP * j0
            u = base
            g_slab, f_slab = zero, zero
            for j1 in range(SIDE):
                hits = counts[j1 * SIDE : (j1 + 1) * SIDE, 0:TILE]
                mass = counts[j1 * SIDE : (j1 + 1) * SIDE, TILE : 2 * TILE]
                one_u = 1.0 + u
                c_u = c_b + u
                inv = 1.0 / (one_u * c_u)
                share = u * one_u * inv
                miss = c_u * inv
                mass_sig = mass * (u * miss)
                grad = hits * share - mass_sig
                info = mass_sig * (share * miss)
                g_slab, f_slab = g_slab + grad, f_slab + info
                g_1 = g_1 + float(AXIS[j1]) * grad
                f_1 = f_1 + float(AXIS[j1]) ** 2 * info
                u = u * ratio1
            g_all, f_all = g_all + g_slab, f_all + f_slab
            g_0, f_0 = g_0 + theta0 * g_slab, f_0 + (theta0 * theta0) * f_slab
            base = base * ratio0
        rest = 1.0 - c
        rows = (g_0, g_1, theta2 * g_all, g_all, f_0, f_1, (theta2 * theta2) * f_all, f_all)
        for j, part in enumerate(rows):
            summed = jnp.sum(part, axis=0, keepdims=True)
            out_ref[j, pl.ds(k, 1), :] = summed if j < 4 else summed * rest
        return carry

    lax.fori_loop(0, count, tile, 0)


def scatter_kernel(items_ref, count_ref, got_ref, out_ref, marg_ref, mean_ref, acc_ref):
    acc_ref[...] = jnp.zeros(acc_ref.shape, F32)
    for b in range(4):
        marg_ref[0:1, b * TILE : (b + 1) * TILE] = got_ref[2 * b, KT : KT + 1, :]
        mean_ref[:, b * TILE : (b + 1) * TILE] = got_ref[2 * b, KT + 1 : KT + 4, :]

        def slot(k, carry):
            row = pl.ds(items_ref[b, k], 1)
            acc_ref[row, :] += got_ref[2 * b, pl.ds(k, 1), :] + got_ref[2 * b + 1, pl.ds(k, 1), :]
            return carry

        lax.fori_loop(0, count_ref[b], slot, 0)
    out_ref[...] = acc_ref[...].astype(BF16)


def local(slopes, intercepts, guessing, responses, tile_items, tile_count):
    takers = lax.axis_size("takers")
    place = lax.axis_index("nodes")
    block, core = place // 2, place % 2
    own = slopes.shape[1]
    blocks = takers * own // TILE
    params = jnp.concatenate([slopes, intercepts[None], guessing[None], jnp.zeros((3, own), BF16)], axis=0)
    mine = lax.dynamic_index_in_dim(params, place, 0, keepdims=False)
    table = lax.all_to_all(jnp.broadcast_to(mine[None], (takers, own)), "takers", 0, 0).reshape(blocks, TILE)
    wanted = jnp.pad(tile_items, ((0, 0), (0, SLOTS - KT)))
    wanted = jnp.repeat(wanted, 2, axis=0).reshape(-1)
    pick = (wanted[:, None] == jnp.arange(blocks, dtype=jnp.int32)[None]).astype(BF16)
    picked = jnp.dot(pick, table, preferred_element_type=F32).astype(BF16).reshape(8, SLOTS, TILE)
    got = lax.all_to_all(picked, "nodes", 0, 0)

    scalars = jnp.stack([block, tile_count[block], core])
    nodes_here = HALF * SIDE * SIDE
    whole = pl.BlockSpec(memory_space=pltpu.VMEM)
    resp_spec = pl.BlockSpec((1, KT, TILE, TILE), lambda i, sc: (sc[0], 0, 0, 0))
    weights, state = pl.pallas_call(
        likelihood_kernel,
        out_shape=(jax.ShapeDtypeStruct((nodes_here, TILE), F32), jax.ShapeDtypeStruct((8, TILE), F32)),
        grid_spec=pltpu.PrefetchScalarGridSpec(
            num_scalar_prefetch=1,
            grid=(1,),
            in_specs=[whole, resp_spec],
            out_specs=(whole, whole),
            scratch_shapes=[
                pltpu.VMEM((8, SLOTS, TILE), F32),
                pltpu.VMEM((nodes_here, 2 * TILE), BF16),
            ],
        ),
        name="likelihood",
    )(scalars, got, responses)
    other = lax.ppermute(state, "nodes", [(i, i ^ 1) for i in range(8)])
    stats = pl.pallas_call(
        statistics_kernel,
        out_shape=jax.ShapeDtypeStruct((8, SLOTS, TILE), F32),
        grid_spec=pltpu.PrefetchScalarGridSpec(
            num_scalar_prefetch=1,
            grid=(1,),
            in_specs=[whole, resp_spec, whole, whole, whole],
            out_specs=whole,
            scratch_shapes=[
                pltpu.VMEM((8, SLOTS, TILE), F32),
                pltpu.VMEM((nodes_here, TILE), BF16),
            ],
        ),
        name="statistics",
    )(scalars, got, responses, weights, state, other)
    partial = lax.all_to_all(stats, "nodes", 0, 0)
    spread, marginal, means = pl.pallas_call(
        scatter_kernel,
        out_shape=(
            jax.ShapeDtypeStruct((blocks, TILE), BF16),
            jax.ShapeDtypeStruct((1, 4 * TILE), F32),
            jax.ShapeDtypeStruct((3, 4 * TILE), F32),
        ),
        grid_spec=pltpu.PrefetchScalarGridSpec(
            num_scalar_prefetch=2,
            grid=(1,),
            in_specs=[whole],
            out_specs=(whole, whole, whole),
            scratch_shapes=[pltpu.VMEM((blocks, TILE), F32)],
        ),
        name="spread",
    )(tile_items, tile_count, partial)
    owned = lax.all_to_all(spread.reshape(takers, own // TILE, TILE), "takers", 0, 0)
    summed = jnp.sum(owned.astype(F32), axis=0)
    all_stats = lax.all_to_all(jnp.broadcast_to(summed[None], (8,) + summed.shape), "nodes", 0, 0)
    all_stats = all_stats.reshape(8, own)
    current = jnp.concatenate([slopes.astype(F32), intercepts.astype(F32)[None]], axis=0)
    new_params = current + all_stats[:4] / (all_stats[4:] + 1.0)
    return new_params, marginal.reshape(-1), means


def solution(mesh):
    in_specs = (
        P(None, "takers"),
        P("takers"),
        P("takers"),
        P("takers", None, None, None),
        P("takers", None),
        P("takers"),
    )
    out_specs = (P(None, "takers"), P("takers"), P(None, "takers"))
    return jax.shard_map(local, mesh=mesh, in_specs=in_specs, out_specs=out_specs, check_vma=False)
```

```python
import math

import jax
import jax.numpy as jnp
import numpy as np
from jax import lax
from jax.experimental import pallas as pl
from jax.experimental.pallas import tpu as pltpu
from jax.sharding import PartitionSpec as P

SIDE = 16
HALF = SIDE // 2
TILE = 128
KT = 12
SLOTS = 16
SLAB = SIDE * SIDE
HERE = HALF * SLAB
F32 = jnp.float32
BF16 = jnp.bfloat16
STEP = 6.0 / 15.0

AXIS = (np.float32(-3.0) + np.float32(6.0) * np.arange(SIDE, dtype=np.float32) / np.float32(15.0)).astype(np.float32)
LOG_TOTAL = 3.0 * math.log(float(np.sum(np.exp(-0.5 * AXIS.astype(np.float64) ** 2))))

VMEM = pl.BlockSpec(memory_space=pltpu.VMEM)
SMEM = pl.BlockSpec(memory_space=pltpu.SMEM)
ANY = pl.BlockSpec(memory_space=pl.ANY)


def params(mib):
    return pltpu.CompilerParams(vmem_limit_bytes=mib << 20)


def axis_column():
    index = lax.broadcasted_iota(jnp.int32, (SIDE, TILE), 0)
    index = jnp.where(index < HALF, index, SIDE + HALF - 1 - index).astype(F32)
    return -3.0 + 6.0 * index / 15.0


def first_theta0(place_ref):
    return -3.0 + STEP * HALF * (place_ref[0] & 1).astype(F32)


def tile_start(par_ref, k, first):
    a0, a1, a2, d, c = (par_ref[j, k : k + 1, :] for j in range(5))
    base = jnp.exp(a2 * axis_column() + (a0 * first + a1 * float(AXIS[0]) + d))
    ratio0 = jnp.broadcast_to(jnp.exp(a0 * STEP), (SIDE, TILE))
    ratio1 = jnp.broadcast_to(jnp.exp(a1 * STEP), (SIDE, TILE))
    return base, ratio0, ratio1, c


def offer_kernel(place_ref, slopes_ref, icpt_ref, guess_ref, out_ref):
    place = place_ref[0]
    slopes = slopes_ref[...].astype(F32)
    row = jnp.where(place == 0, slopes[0:1], jnp.where(place == 1, slopes[1:2], slopes[2:3]))
    rows = jnp.concatenate([row[:, j * TILE : (j + 1) * TILE] for j in range(row.shape[1] // TILE)], axis=0)
    rows = jnp.where(place == 3, icpt_ref[...].astype(F32), rows)
    rows = jnp.where(place >= 4, guess_ref[...].astype(F32), rows)
    out_ref[...] = jnp.broadcast_to(rows.astype(BF16)[None], out_ref.shape)


def marks_kernel(place_ref, count_ref, resp_ref, first_ref, second_ref, buf_ref, sem_ref):
    block = place_ref[0] >> 1
    copies = [pltpu.make_async_copy(resp_ref.at[block, k], buf_ref.at[k], sem_ref.at[k]) for k in range(KT)]
    for copy in copies:
        copy.start()
    count = count_ref[block]
    for k, copy in enumerate(copies):
        copy.wait()
        codes = jnp.where(k < count, buf_ref[k], 0)
        second_ref[k, :, 0:TILE] = (codes == 2).astype(BF16)
        second_ref[k, :, TILE : 2 * TILE] = (codes > 0).astype(BF16)
        turned = jnp.transpose(codes.astype(F32))
        first_ref[2 * k] = (turned == 2.0).astype(BF16)
        first_ref[2 * k + 1] = (turned == 1.0).astype(BF16)


def pick_kernel(items_ref, table_ref, out_ref, wide_ref, rows_ref):
    wide_ref[...] = table_ref[...].astype(F32)
    last = wide_ref.shape[0] - 1
    for b in range(4):
        rows_ref[b, KT:SLOTS, :] = jnp.zeros((SLOTS - KT, TILE), F32)
        for k in range(KT):
            item = jnp.minimum(jnp.maximum(items_ref[b, k], 0), last)
            rows_ref[b, k : k + 1, :] = wide_ref[pl.ds(item, 1), :]
    for b in range(4):
        rows = rows_ref[b].astype(BF16)
        out_ref[2 * b] = rows
        out_ref[2 * b + 1] = rows


def likelihood_kernel(place_ref, got_ref, marks_ref, w_ref, st_ref, par_ref, tab_a, tab_b):
    first = first_theta0(place_ref)
    par_ref[...] = got_ref[...].astype(F32)
    theta2 = axis_column()
    half_square = -0.5 * (theta2 * theta2)
    for j0 in range(HALF):
        theta0 = first + STEP * j0
        for j1 in range(SIDE):
            rows = pl.ds((j0 * SIDE + j1) * SIDE, SIDE)
            w_ref[rows, :] = half_square - (0.5 * (theta0 * theta0) + (0.5 * float(AXIS[j1]) ** 2 + LOG_TOTAL))

    def tables(k, tab_ref, at):
        base, ratio0, ratio1, c = tile_start(par_ref, k, first)
        c_b = jnp.broadcast_to(c, (SIDE, TILE))
        log_rest = jnp.broadcast_to(jnp.log(1.0 - c), (SIDE, TILE))
        for j0 in range(HALF):
            u = base
            for j1 in range(SIDE):
                rows = pl.ds((j0 * SIDE + j1) * SIDE, SIDE)
                log_one = jnp.log(1.0 + u)
                tab_ref[rows, at : at + TILE] = (jnp.log(c_b + u) - log_one).astype(BF16)
                tab_ref[rows, at + TILE : at + 2 * TILE] = (log_rest - log_one).astype(BF16)
                u = u * ratio1
            base = base * ratio0

    def gather(pair, tab_ref):
        marks = marks_ref[pl.ds(4 * pair, 4)].reshape(4 * TILE, TILE)
        for s in range(0, HERE, 2 * SLAB):
            w_ref[s : s + 2 * SLAB, :] += jnp.dot(tab_ref[s : s + 2 * SLAB, :], marks, preferred_element_type=F32)

    for pair in range(KT // 2):
        tab_ref = (tab_a, tab_b)[pair % 2]
        for side in range(2):
            tables(2 * pair + side, tab_ref, 2 * TILE * side)
        if pair:
            gather(pair - 1, (tab_a, tab_b)[1 - pair % 2])
    gather(KT // 2 - 1, (tab_a, tab_b)[(KT // 2 - 1) % 2])

    top = jnp.full((SIDE, TILE), -jnp.inf, F32)
    for j in range(HALF * SIDE):
        top = jnp.maximum(top, w_ref[j * SIDE : (j + 1) * SIDE, :])
    top = jnp.max(top, axis=0, keepdims=True)
    total = jnp.zeros((SIDE, TILE), F32)
    mom0 = jnp.zeros((SIDE, TILE), F32)
    mom1 = jnp.zeros((SIDE, TILE), F32)
    for j0 in range(HALF):
        slab_sum = jnp.zeros((SIDE, TILE), F32)
        for j1 in range(SIDE):
            rows = pl.ds((j0 * SIDE + j1) * SIDE, SIDE)
            w = jnp.exp(w_ref[rows, :] - top)
            w_ref[rows, :] = w
            slab_sum = slab_sum + w
            mom1 = mom1 + float(AXIS[j1]) * w
        total = total + slab_sum
        mom0 = mom0 + (first + STEP * j0) * slab_sum
    st_ref[0:1, :] = top
    for j, part in enumerate((total, mom0, mom1, total * theta2)):
        st_ref[j + 1 : j + 2, :] = jnp.sum(part, axis=0, keepdims=True)
    st_ref[5:8, :] = jnp.zeros((3, TILE), F32)


def statistics_kernel(place_ref, got_ref, marks_ref, w_ref, mine_ref, other_ref, out_ref, par_ref, post_ref):
    first = first_theta0(place_ref)
    par_ref[...] = got_ref[...].astype(F32)
    mine, other = mine_ref[...], other_ref[...]
    top = jnp.maximum(mine[0:1], other[0:1])
    both = mine[1:5] * jnp.exp(mine[0:1] - top) + other[1:5] * jnp.exp(other[0:1] - top)
    log_norm = top + jnp.log(both[0:1])
    means = both[1:4] / both[0:1]
    scale = jnp.exp(mine[0:1] - log_norm)
    post_ref[...] = (w_ref[...] * scale).astype(BF16)
    for j in range(8):
        out_ref[j, KT : KT + 1, :] = log_norm
        out_ref[j, KT + 1 : KT + 4, :] = means
    theta2 = axis_column()
    zero = jnp.zeros((SIDE, TILE), F32)
    zero_h = jnp.zeros((HALF, TILE), F32)

    def tile(k):
        marks = marks_ref[k]
        a0, a1, a2, d, c = (par_ref[j, pl.ds(k, 1), :] for j in range(5))
        base = jnp.exp(a2 * theta2 + (a0 * first + a1 * float(AXIS[0]) + d))
        ratio0 = jnp.broadcast_to(jnp.exp(a0 * STEP), (SIDE, TILE))
        ratio1 = jnp.broadcast_to(jnp.exp(a1 * STEP), (SIDE, TILE))
        c_b = jnp.broadcast_to(c, (SIDE, TILE))
        g_all, g_0, g_run = zero, zero, zero_h
        f_all, f_0, f_1 = zero_h, zero_h, zero_h
        for j0 in range(HALF):
            counts = jnp.dot(post_ref[j0 * SLAB : (j0 + 1) * SLAB, :], marks, preferred_element_type=F32)
            theta0 = first + STEP * j0
            u = base
            g_slab, f_slab = zero, zero_h
            for j1 in range(SIDE):
                hits = counts[j1 * SIDE : (j1 + 1) * SIDE, 0:TILE]
                mass = counts[j1 * SIDE : (j1 + 1) * SIDE, TILE : 2 * TILE]
                miss = 1.0 / (1.0 + u)
                share = u * (1.0 / (c_b + u))
                mass_sig = mass * (u * miss)
                info = mass_sig * (share * miss)
                g_slab = g_slab + (hits * share - mass_sig)
                g_run = g_run + (g_slab[:HALF] + g_slab[HALF:])
                info = info[:HALF] + info[HALF:]
                f_slab = f_slab + info
                f_1 = f_1 + float(AXIS[j1]) ** 2 * info
                u = u * ratio1
            g_all, f_all = g_all + g_slab, f_all + f_slab
            g_0, f_0 = g_0 + theta0 * g_slab, f_0 + (theta0 * theta0) * f_slab
            base = base * ratio0
        square = theta2[:HALF] * theta2[:HALF]
        g_sum = g_all[:HALF] + g_all[HALF:]
        g_1 = (float(AXIS[-1]) + STEP) * g_sum - STEP * g_run
        rest = 1.0 - c
        rows = (g_0, g_1, theta2 * g_all, g_sum, f_0, f_1, square * f_all, f_all)
        for j, part in enumerate(rows):
            summed = jnp.sum(part, axis=0, keepdims=True)
            out_ref[j, pl.ds(k, 1), :] = summed if j < 4 else summed * rest

    @pl.loop(0, KT // 2)
    def _(pair):
        tile(2 * pair)
        tile(2 * pair + 1)


def spread_kernel(items_ref, count_ref, got_ref, out_ref, marg_ref, mean_ref, acc_ref):
    acc_ref[...] = jnp.zeros(acc_ref.shape, F32)
    last = acc_ref.shape[0] - 1
    for b in range(4):
        marg_ref[0:1, b * TILE : (b + 1) * TILE] = got_ref[2 * b, KT : KT + 1, :]
        mean_ref[:, b * TILE : (b + 1) * TILE] = got_ref[2 * b, KT + 1 : KT + 4, :]
        both = got_ref[2 * b] + got_ref[2 * b + 1]
        for k in range(KT):
            row = pl.ds(jnp.minimum(jnp.maximum(items_ref[b, k], 0), last), 1)
            acc_ref[row, :] += both[k : k + 1]
    out_ref[...] = acc_ref[...].astype(BF16)


def gather_kernel(got_ref, out_ref):
    total = jnp.sum(got_ref[...].astype(F32), axis=0)
    out_ref[...] = jnp.broadcast_to(total[None], out_ref.shape)


def shape(dims, kind=F32):
    return jax.ShapeDtypeStruct(dims, kind)


def local(slopes, intercepts, guessing, responses, tile_items, tile_count):
    takers = lax.axis_size("takers")
    place = lax.axis_index("nodes").reshape(1)
    own = slopes.shape[1]
    rows = own // TILE
    blocks = takers * rows
    offer = pl.pallas_call(
        offer_kernel,
        out_shape=shape((takers, rows, TILE), BF16),
        in_specs=[SMEM, VMEM, VMEM, VMEM],
        out_specs=VMEM,
        compiler_params=params(4),
        name="offer",
    )(place, slopes, intercepts.reshape(rows, TILE), guessing.reshape(rows, TILE))
    marks1, marks2 = pl.pallas_call(
        marks_kernel,
        out_shape=(shape((2 * KT, TILE, TILE), BF16), shape((KT, TILE, 2 * TILE), BF16)),
        in_specs=[SMEM, SMEM, ANY],
        out_specs=(VMEM, VMEM),
        scratch_shapes=[pltpu.VMEM((KT, TILE, TILE), jnp.int32), pltpu.SemaphoreType.DMA((KT,))],
        compiler_params=params(6),
        name="marks",
    )(place, tile_count, responses)
    table = lax.all_to_all(offer, "takers", 0, 0).reshape(blocks, TILE)
    picked = pl.pallas_call(
        pick_kernel,
        out_shape=shape((8, SLOTS, TILE), BF16),
        in_specs=[SMEM, VMEM],
        out_specs=VMEM,
        scratch_shapes=[pltpu.VMEM((blocks, TILE), F32), pltpu.VMEM((4, SLOTS, TILE), F32)],
        compiler_params=params(4),
        name="pick",
    )(tile_items, table)
    got = lax.all_to_all(picked, "nodes", 0, 0)
    weights, state = pl.pallas_call(
        likelihood_kernel,
        out_shape=(shape((HERE, TILE)), shape((8, TILE))),
        in_specs=[SMEM, VMEM, VMEM],
        out_specs=(VMEM, VMEM),
        scratch_shapes=[
            pltpu.VMEM((8, SLOTS, TILE), F32),
            pltpu.VMEM((HERE, 4 * TILE), BF16),
            pltpu.VMEM((HERE, 4 * TILE), BF16),
        ],
        compiler_params=params(14),
        name="likelihood",
    )(place, got, marks1)
    other = lax.ppermute(state, "nodes", [(i, i ^ 1) for i in range(8)])
    stats = pl.pallas_call(
        statistics_kernel,
        out_shape=shape((8, SLOTS, TILE)),
        in_specs=[SMEM, VMEM, VMEM, VMEM, VMEM, VMEM],
        out_specs=VMEM,
        scratch_shapes=[pltpu.VMEM((8, SLOTS, TILE), F32), pltpu.VMEM((HERE, TILE), BF16)],
        compiler_params=params(14),
        name="statistics",
    )(place, got, marks2, weights, state, other)
    partial = lax.all_to_all(stats, "nodes", 0, 0)
    spread, marginal, means = pl.pallas_call(
        spread_kernel,
        out_shape=(shape((blocks, TILE), BF16), shape((1, 4 * TILE)), shape((3, 4 * TILE))),
        in_specs=[SMEM, SMEM, VMEM],
        out_specs=(VMEM, VMEM, VMEM),
        scratch_shapes=[pltpu.VMEM((blocks, TILE), F32)],
        compiler_params=params(4),
        name="spread",
    )(tile_items, tile_count, partial)
    owned = lax.all_to_all(spread.reshape(takers, rows, TILE), "takers", 0, 0)
    summed = pl.pallas_call(
        gather_kernel,
        out_shape=shape((8, rows, TILE)),
        in_specs=[VMEM],
        out_specs=VMEM,
        compiler_params=params(4),
        name="gather",
    )(owned)
    all_stats = lax.all_to_all(summed, "nodes", 0, 0).reshape(8, own)
    current = jnp.concatenate([slopes.astype(F32), intercepts.astype(F32)[None]], axis=0)
    new_params = current + all_stats[:4] / (all_stats[4:] + 1.0)
    return new_params, marginal.reshape(-1), means


def solution(mesh):
    in_specs = (
        P(None, "takers"),
        P("takers"),
        P("takers"),
        P("takers", None, None, None),
        P("takers", None),
        P("takers"),
    )
    out_specs = (P(None, "takers"), P("takers"), P(None, "takers"))
    return jax.shard_map(local, mesh=mesh, in_specs=in_specs, out_specs=out_specs, check_vma=False)
```

```python
import math

import jax
import jax.numpy as jnp
import numpy as np
from jax import lax
from jax.experimental import pallas as pl
from jax.experimental.pallas import tpu as pltpu
from jax.sharding import PartitionSpec as P

SIDE = 16
HALF = SIDE // 2
TILE = 128
KT = 12
SLOTS = 16
SLAB = SIDE * SIDE
HERE = HALF * SLAB
F32 = jnp.float32
BF16 = jnp.bfloat16
STEP = 6.0 / 15.0

AXIS = (np.float32(-3.0) + np.float32(6.0) * np.arange(SIDE, dtype=np.float32) / np.float32(15.0)).astype(np.float32)
LOG_TOTAL = 3.0 * math.log(float(np.sum(np.exp(-0.5 * AXIS.astype(np.float64) ** 2))))

VMEM = pl.BlockSpec(memory_space=pltpu.VMEM)
SMEM = pl.BlockSpec(memory_space=pltpu.SMEM)
HBM = pl.BlockSpec(memory_space=pltpu.HBM)


def params(mib):
    return pltpu.CompilerParams(vmem_limit_bytes=mib << 20)


def axis_column():
    index = lax.broadcasted_iota(jnp.int32, (SIDE, TILE), 0)
    index = jnp.where(index < HALF, index, SIDE + HALF - 1 - index).astype(F32)
    return -3.0 + 6.0 * index / 15.0


def first_theta0(place_ref):
    return -3.0 + STEP * HALF * (place_ref[0] & 1).astype(F32)


def tile_start(par_ref, k, first):
    a0, a1, a2, d, c = (par_ref[j, pl.ds(k, 1), :] for j in range(5))
    base = jnp.exp(a2 * axis_column() + (a0 * first + a1 * float(AXIS[0]) + d))
    ratio0 = jnp.broadcast_to(jnp.exp(a0 * STEP), (SIDE, TILE))
    ratio1 = jnp.broadcast_to(jnp.exp(a1 * STEP), (SIDE, TILE))
    return base, ratio0, ratio1, c


def offer_kernel(place_ref, slopes_hbm, icpt_hbm, guess_hbm, out_ref, slopes_ref, icpt_ref, guess_ref, sem_ref):
    copies = [
        pltpu.make_async_copy(slopes_hbm, slopes_ref, sem_ref.at[0]),
        pltpu.make_async_copy(icpt_hbm, icpt_ref, sem_ref.at[1]),
        pltpu.make_async_copy(guess_hbm, guess_ref, sem_ref.at[2]),
    ]
    for copy in copies:
        copy.start()
    for copy in copies:
        copy.wait()
    place = place_ref[0]
    slopes = slopes_ref[...].astype(F32)
    row = jnp.where(place == 0, slopes[0:1], jnp.where(place == 1, slopes[1:2], slopes[2:3]))
    rows = jnp.concatenate([row[:, j * TILE : (j + 1) * TILE] for j in range(row.shape[1] // TILE)], axis=0)
    rows = jnp.where(place == 3, icpt_ref[...].astype(F32), rows)
    rows = jnp.where(place >= 4, guess_ref[...].astype(F32), rows)
    out_ref[...] = jnp.broadcast_to(rows.astype(BF16)[None], out_ref.shape)


def plan_kernel(count_ref, items_ref, pick_ref, turn_ref, wide_ref):
    wide_ref[...] = jnp.zeros(wide_ref.shape, F32)
    blocks = wide_ref.shape[1]
    block_of = lax.broadcasted_iota(jnp.int32, (1, blocks), 1)
    for b in range(4):
        for k in range(KT):
            at = b * SLOTS + k
            wide_ref[at : at + 1, :] = (block_of == items_ref[b, k]).astype(F32)
            at += 4 * SLOTS
            wide_ref[at : at + 1, 0:TILE] = jnp.full((1, TILE), k < count_ref[b]).astype(F32)
    pick_ref[...] = wide_ref[...].astype(BF16)
    for j in range(blocks // TILE):
        turn_ref[j * TILE : (j + 1) * TILE, :] = jnp.transpose(wide_ref[:, j * TILE : (j + 1) * TILE]).astype(BF16)


def pick_kernel(place_ref, block_ref, pick_ref, table_ref, out_ref):
    rows = jnp.dot(pick_ref[0 : 4 * SLOTS, :], table_ref[...], preferred_element_type=F32)
    live = pick_ref[4 * SLOTS : 8 * SLOTS, 0:TILE].astype(F32)
    rows = jnp.where(place_ref[0] == 5, live, rows).astype(BF16)
    for b in range(4):
        out_ref[2 * b] = rows[b * SLOTS : (b + 1) * SLOTS]
        out_ref[2 * b + 1] = rows[b * SLOTS : (b + 1) * SLOTS]


def likelihood_kernel(place_ref, got_ref, resp_ref, w_ref, st_ref, par_ref, tab_a, tab_b, mark_a, mark_b):
    first = first_theta0(place_ref)
    par_ref[...] = got_ref[...].astype(F32)
    theta2 = axis_column()
    half_square = -0.5 * (theta2 * theta2)
    for j0 in range(HALF):
        theta0 = first + STEP * j0
        for j1 in range(SIDE):
            rows = pl.ds((j0 * SIDE + j1) * SIDE, SIDE)
            w_ref[rows, :] = half_square - (0.5 * (theta0 * theta0) + (0.5 * float(AXIS[j1]) ** 2 + LOG_TOTAL))

    def tables(k, tab_ref, at):
        base, ratio0, ratio1, c = tile_start(par_ref, k, first)
        c_b = jnp.broadcast_to(c, (SIDE, TILE))
        log_rest = jnp.broadcast_to(jnp.log(1.0 - c), (SIDE, TILE))
        for j0 in range(HALF):
            u = base
            for j1 in range(SIDE):
                rows = pl.ds((j0 * SIDE + j1) * SIDE, SIDE)
                log_one = jnp.log(1.0 + u)
                tab_ref[rows, at : at + TILE] = (jnp.log(c_b + u) - log_one).astype(BF16)
                tab_ref[rows, at + TILE : at + 2 * TILE] = (log_rest - log_one).astype(BF16)
                u = u * ratio1
            base = base * ratio0

    def mark(k, mark_ref, at):
        codes = jnp.transpose(resp_ref[k].astype(F32))
        live = par_ref[5, pl.ds(k, 1), :]
        mark_ref[at : at + TILE, :] = jnp.where(codes == 2.0, live, 0.0).astype(BF16)
        mark_ref[at + TILE : at + 2 * TILE, :] = jnp.where(codes == 1.0, live, 0.0).astype(BF16)

    def gather(tab_ref, mark_ref):
        marks = mark_ref[...]
        for s in range(0, HERE, 4 * SLAB):
            w_ref[s : s + 4 * SLAB, :] += jnp.dot(tab_ref[s : s + 4 * SLAB, :], marks, preferred_element_type=F32)

    def both(step, carry):
        for half, (tab_ref, mark_ref) in enumerate(((tab_a, mark_a), (tab_b, mark_b))):
            for side in range(2):
                k = 4 * step + 2 * half + side
                mark(k, mark_ref, 2 * TILE * side)
                tables(k, tab_ref, 2 * TILE * side)
            gather(*((tab_b, mark_b), (tab_a, mark_a))[half])
        return carry

    tab_b[...] = jnp.zeros(tab_b.shape, BF16)
    mark_b[...] = jnp.zeros(mark_b.shape, BF16)
    lax.fori_loop(0, KT // 4, both, 0)
    gather(tab_b, mark_b)

    top = jnp.full((SIDE, TILE), -jnp.inf, F32)
    for j in range(HALF * SIDE):
        top = jnp.maximum(top, w_ref[j * SIDE : (j + 1) * SIDE, :])
    top = jnp.max(top, axis=0, keepdims=True)
    total = jnp.zeros((SIDE, TILE), F32)
    mom0 = jnp.zeros((SIDE, TILE), F32)
    mom1 = jnp.zeros((SIDE, TILE), F32)
    for j0 in range(HALF):
        slab_sum = jnp.zeros((SIDE, TILE), F32)
        for j1 in range(SIDE):
            rows = pl.ds((j0 * SIDE + j1) * SIDE, SIDE)
            w = jnp.exp(w_ref[rows, :] - top)
            w_ref[rows, :] = w
            slab_sum = slab_sum + w
            mom1 = mom1 + float(AXIS[j1]) * w
        total = total + slab_sum
        mom0 = mom0 + (first + STEP * j0) * slab_sum
    st_ref[0:1, :] = top
    for j, part in enumerate((total, mom0, mom1, total * theta2)):
        st_ref[j + 1 : j + 2, :] = jnp.sum(part, axis=0, keepdims=True)
    st_ref[5:8, :] = jnp.zeros((3, TILE), F32)


def statistics_kernel(place_ref, got_ref, resp_ref, w_ref, mine_ref, other_ref, out_ref, par_ref, post_ref):
    first = first_theta0(place_ref)
    par_ref[...] = got_ref[...].astype(F32)
    mine, other = mine_ref[...], other_ref[...]
    top = jnp.maximum(mine[0:1], other[0:1])
    both = mine[1:5] * jnp.exp(mine[0:1] - top) + other[1:5] * jnp.exp(other[0:1] - top)
    log_norm = top + jnp.log(both[0:1])
    means = both[1:4] / both[0:1]
    scale = jnp.exp(mine[0:1] - log_norm)
    post_ref[...] = (w_ref[...] * scale).astype(BF16)
    for j in range(8):
        out_ref[j, KT : KT + 1, :] = log_norm
        out_ref[j, KT + 1 : KT + 4, :] = means
    theta2 = axis_column()
    zero = jnp.zeros((SIDE, TILE), F32)
    zero_h = jnp.zeros((HALF, TILE), F32)

    def tile(k):
        a0, a1, a2, d, c, live = (par_ref[j, pl.ds(k, 1), :] for j in range(6))
        codes = resp_ref[k]
        hit, any_answer = jnp.where(codes == 2, live, 0.0), jnp.where(codes > 0, live, 0.0)
        marks = jnp.concatenate([hit.astype(BF16), any_answer.astype(BF16)], axis=1)
        base = jnp.exp(a2 * theta2 + (a0 * first + a1 * float(AXIS[0]) + d))
        ratio0 = jnp.broadcast_to(jnp.exp(a0 * STEP), (SIDE, TILE))
        ratio1 = jnp.broadcast_to(jnp.exp(a1 * STEP), (SIDE, TILE))
        c_b = jnp.broadcast_to(c, (SIDE, TILE))
        g_all, g_0, g_run = zero, zero, zero_h
        f_all, f_0, f_1 = zero_h, zero_h, zero_h
        for j0 in range(HALF):
            counts = jnp.dot(post_ref[j0 * SLAB : (j0 + 1) * SLAB, :], marks, preferred_element_type=F32)
            theta0 = first + STEP * j0
            u = base
            g_slab, f_slab = zero, zero_h
            for j1 in range(SIDE):
                hits = counts[j1 * SIDE : (j1 + 1) * SIDE, 0:TILE]
                mass = counts[j1 * SIDE : (j1 + 1) * SIDE, TILE : 2 * TILE]
                miss = 1.0 / (1.0 + u)
                share = u * (1.0 / (c_b + u))
                mass_sig = mass * (u * miss)
                info = mass_sig * (share * miss)
                g_slab = g_slab + (hits * share - mass_sig)
                g_run = g_run + (g_slab[:HALF] + g_slab[HALF:])
                info = info[:HALF] + info[HALF:]
                f_slab = f_slab + info
                f_1 = f_1 + float(AXIS[j1]) ** 2 * info
                u = u * ratio1
            g_all, f_all = g_all + g_slab, f_all + f_slab
            g_0, f_0 = g_0 + theta0 * g_slab, f_0 + (theta0 * theta0) * f_slab
            base = base * ratio0
        square = theta2[:HALF] * theta2[:HALF]
        g_sum = g_all[:HALF] + g_all[HALF:]
        g_1 = (float(AXIS[-1]) + STEP) * g_sum - STEP * g_run
        rest = 1.0 - c
        rows = (g_0, g_1, theta2 * g_all, g_sum, f_0, f_1, square * f_all, f_all)
        for j, part in enumerate(rows):
            summed = jnp.sum(part, axis=0, keepdims=True)
            out_ref[j, pl.ds(k, 1), :] = summed if j < 4 else summed * rest

    @pl.loop(0, KT // 4)
    def _(step):
        for side in range(4):
            tile(4 * step + side)


def spread_kernel(turn_ref, got_ref, out_ref, marg_ref, mean_ref):
    both = []
    for b in range(4):
        marg_ref[0:1, b * TILE : (b + 1) * TILE] = got_ref[2 * b, KT : KT + 1, :]
        mean_ref[:, b * TILE : (b + 1) * TILE] = got_ref[2 * b, KT + 1 : KT + 4, :]
        both.append(got_ref[2 * b] + got_ref[2 * b + 1])
    both.extend([jnp.zeros((4 * SLOTS, TILE), F32)])
    both = jnp.concatenate(both, axis=0)
    high = both.astype(BF16)
    low = (both - high.astype(F32)).astype(BF16)
    turn = turn_ref[...]
    total = jnp.dot(turn, high, preferred_element_type=F32) + jnp.dot(turn, low, preferred_element_type=F32)
    out_ref[...] = total.astype(BF16)


def gather_kernel(got_ref, out_ref):
    total = jnp.sum(got_ref[...].astype(F32), axis=0)
    out_ref[...] = jnp.broadcast_to(total[None], out_ref.shape)


def update_kernel(slopes_ref, icpt_ref, got_ref, out_ref):
    slopes = slopes_ref[...].astype(F32)
    icpt = icpt_ref[...].astype(F32)
    for p in range(4):
        step = got_ref[p] / (got_ref[p + 4] + 1.0)
        for j in range(step.shape[0]):
            span = slice(j * TILE, (j + 1) * TILE)
            now = slopes[p : p + 1, span] if p < 3 else icpt[j : j + 1]
            out_ref[p : p + 1, span] = now + step[j : j + 1]


def shape(dims, kind=F32):
    return jax.ShapeDtypeStruct(dims, kind)


def local(slopes, intercepts, guessing, responses, tile_items, tile_count):
    takers = lax.axis_size("takers")
    place = lax.axis_index("nodes").reshape(1)
    block = place >> 1
    own = slopes.shape[1]
    rows = own // TILE
    blocks = takers * rows
    icpt, guess = intercepts.reshape(rows, TILE), guessing.reshape(rows, TILE)
    offer = pl.pallas_call(
        offer_kernel,
        out_shape=shape((takers, rows, TILE), BF16),
        in_specs=[SMEM, HBM, HBM, HBM],
        out_specs=VMEM,
        scratch_shapes=[
            pltpu.VMEM((3, own), BF16),
            pltpu.VMEM((rows, TILE), BF16),
            pltpu.VMEM((rows, TILE), BF16),
            pltpu.SemaphoreType.DMA((3,)),
        ],
        compiler_params=params(60),
        name="offer",
    )(place, slopes, icpt, guess)
    pick, turn = pl.pallas_call(
        plan_kernel,
        out_shape=(shape((TILE, blocks), BF16), shape((blocks, TILE), BF16)),
        in_specs=[SMEM, SMEM],
        out_specs=(VMEM, VMEM),
        scratch_shapes=[pltpu.VMEM((TILE, blocks), F32)],
        compiler_params=params(6),
        name="plan",
    )(tile_count, tile_items)
    table = lax.all_to_all(offer, "takers", 0, 0).reshape(blocks, TILE)
    picked = pl.pallas_call(
        pick_kernel,
        out_shape=shape((8, SLOTS, TILE), BF16),
        in_specs=[SMEM, SMEM, VMEM, VMEM],
        out_specs=VMEM,
        compiler_params=params(4),
        name="pick",
    )(place, block, pick, table)
    got, block = lax.optimization_barrier((lax.all_to_all(picked, "nodes", 0, 0), block))
    answers = lax.dynamic_index_in_dim(responses, block[0], 0, keepdims=False)
    weights, state = pl.pallas_call(
        likelihood_kernel,
        out_shape=(shape((HERE, TILE)), shape((8, TILE))),
        in_specs=[SMEM, VMEM, VMEM],
        out_specs=(VMEM, VMEM),
        scratch_shapes=[
            pltpu.VMEM((8, SLOTS, TILE), F32),
            pltpu.VMEM((HERE, 4 * TILE), BF16),
            pltpu.VMEM((HERE, 4 * TILE), BF16),
            pltpu.VMEM((4 * TILE, TILE), BF16),
            pltpu.VMEM((4 * TILE, TILE), BF16),
        ],
        compiler_params=params(14),
        name="likelihood",
    )(place, got, answers)
    other = lax.ppermute(state, "nodes", [(i, i ^ 1) for i in range(8)])
    stats = pl.pallas_call(
        statistics_kernel,
        out_shape=shape((8, SLOTS, TILE)),
        in_specs=[SMEM, VMEM, VMEM, VMEM, VMEM, VMEM],
        out_specs=VMEM,
        scratch_shapes=[pltpu.VMEM((8, SLOTS, TILE), F32), pltpu.VMEM((HERE, TILE), BF16)],
        compiler_params=params(14),
        name="statistics",
    )(place, got, answers, weights, state, other)
    partial = lax.all_to_all(stats, "nodes", 0, 0)
    spread, marginal, means = pl.pallas_call(
        spread_kernel,
        out_shape=(shape((blocks, TILE), BF16), shape((1, 4 * TILE)), shape((3, 4 * TILE))),
        in_specs=[VMEM, VMEM],
        out_specs=(VMEM, VMEM, VMEM),
        compiler_params=params(4),
        name="spread",
    )(turn, partial)
    owned = lax.all_to_all(spread.reshape(takers, rows, TILE), "takers", 0, 0)
    summed = pl.pallas_call(
        gather_kernel,
        out_shape=shape((8, rows, TILE)),
        in_specs=[VMEM],
        out_specs=VMEM,
        compiler_params=params(4),
        name="gather",
    )(owned)
    new_params = pl.pallas_call(
        update_kernel,
        out_shape=shape((4, own)),
        in_specs=[VMEM, VMEM, VMEM],
        out_specs=VMEM,
        compiler_params=params(4),
        name="update",
    )(slopes, icpt, lax.all_to_all(summed, "nodes", 0, 0))
    return new_params, marginal.reshape(-1), means


def solution(mesh):
    in_specs = (
        P(None, "takers"),
        P("takers"),
        P("takers"),
        P("takers", None, None, None),
        P("takers", None),
        P("takers"),
    )
    out_specs = (P(None, "takers"), P("takers"), P(None, "takers"))
    return jax.shard_map(local, mesh=mesh, in_specs=in_specs, out_specs=out_specs, check_vma=False)
```

```python
import math

import jax
import jax.numpy as jnp
import numpy as np
from jax import lax
from jax.experimental import pallas as pl
from jax.experimental.pallas import tpu as pltpu
from jax.sharding import PartitionSpec as P

SIDE = 16
HALF = SIDE // 2
TILE = 128
KT = 12
SLOTS = 16
SLAB = SIDE * SIDE
HERE = HALF * SLAB
F32 = jnp.float32
BF16 = jnp.bfloat16
STEP = 6.0 / 15.0

AXIS = (np.float32(-3.0) + np.float32(6.0) * np.arange(SIDE, dtype=np.float32) / np.float32(15.0)).astype(np.float32)
LOG_TOTAL = 3.0 * math.log(float(np.sum(np.exp(-0.5 * AXIS.astype(np.float64) ** 2))))

VMEM = pl.BlockSpec(memory_space=pltpu.VMEM)
SMEM = pl.BlockSpec(memory_space=pltpu.SMEM)
HBM = pl.BlockSpec(memory_space=pltpu.HBM)


def params(mib):
    return pltpu.CompilerParams(vmem_limit_bytes=mib << 20)


def axis_column():
    index = lax.broadcasted_iota(jnp.int32, (SIDE, TILE), 0)
    index = jnp.where(index < HALF, index, SIDE + HALF - 1 - index).astype(F32)
    return -3.0 + 6.0 * index / 15.0


def first_theta0(place_ref):
    return -3.0 + STEP * HALF * (place_ref[0] & 1).astype(F32)


def tile_start(par_ref, k, first):
    a0, a1, a2, d, c = (par_ref[j, pl.ds(k, 1), :] for j in range(5))
    base = jnp.exp(a2 * axis_column() + (a0 * first + a1 * float(AXIS[0]) + d))
    ratio0 = jnp.broadcast_to(jnp.exp(a0 * STEP), (SIDE, TILE))
    ratio1 = jnp.broadcast_to(jnp.exp(a1 * STEP), (SIDE, TILE))
    return base, ratio0, ratio1, c


def offer_kernel(place_ref, slopes_hbm, icpt_hbm, guess_hbm, out_ref, slopes_ref, icpt_ref, guess_ref, sem_ref):
    copies = [
        pltpu.make_async_copy(slopes_hbm, slopes_ref, sem_ref.at[0]),
        pltpu.make_async_copy(icpt_hbm, icpt_ref, sem_ref.at[1]),
        pltpu.make_async_copy(guess_hbm, guess_ref, sem_ref.at[2]),
    ]
    for copy in copies:
        copy.start()
    for copy in copies:
        copy.wait()
    place = place_ref[0]
    slopes = slopes_ref[...].astype(F32)
    row = jnp.where(place == 0, slopes[0:1], jnp.where(place == 1, slopes[1:2], slopes[2:3]))
    rows = jnp.concatenate([row[:, j * TILE : (j + 1) * TILE] for j in range(row.shape[1] // TILE)], axis=0)
    rows = jnp.where(place == 3, icpt_ref[...].astype(F32), rows)
    rows = jnp.where(place >= 4, guess_ref[...].astype(F32), rows)
    out_ref[...] = jnp.broadcast_to(rows.astype(BF16)[None], out_ref.shape)


def plan_kernel(count_ref, items_ref, pick_ref, turn_ref, wide_ref):
    wide_ref[...] = jnp.zeros(wide_ref.shape, F32)
    blocks = wide_ref.shape[1]
    block_of = lax.broadcasted_iota(jnp.int32, (1, blocks), 1)
    for b in range(4):
        for k in range(KT):
            at = b * SLOTS + k
            wide_ref[at : at + 1, :] = (block_of == items_ref[b, k]).astype(F32)
            at += 4 * SLOTS
            wide_ref[at : at + 1, 0:TILE] = jnp.full((1, TILE), k < count_ref[b]).astype(F32)
    pick_ref[...] = wide_ref[...].astype(BF16)
    for j in range(blocks // TILE):
        turn_ref[j * TILE : (j + 1) * TILE, :] = jnp.transpose(wide_ref[:, j * TILE : (j + 1) * TILE]).astype(BF16)


def pick_kernel(place_ref, block_ref, pick_ref, table_ref, out_ref):
    rows = jnp.dot(pick_ref[0 : 4 * SLOTS, :], table_ref[...], preferred_element_type=F32)
    live = pick_ref[4 * SLOTS : 8 * SLOTS, 0:TILE].astype(F32)
    rows = jnp.where(place_ref[0] == 5, live, rows).astype(BF16)
    for b in range(4):
        out_ref[2 * b] = rows[b * SLOTS : (b + 1) * SLOTS]
        out_ref[2 * b + 1] = rows[b * SLOTS : (b + 1) * SLOTS]


def likelihood_kernel(place_ref, got_ref, resp_ref, w_ref, st_ref, par_ref, tab_a, tab_b, mark_a, mark_b):
    first = first_theta0(place_ref)
    par_ref[...] = got_ref[...].astype(F32)
    theta2 = axis_column()
    half_square = -0.5 * (theta2 * theta2)
    for j0 in range(HALF):
        theta0 = first + STEP * j0
        for j1 in range(SIDE):
            rows = pl.ds((j0 * SIDE + j1) * SIDE, SIDE)
            w_ref[rows, :] = half_square - (0.5 * (theta0 * theta0) + (0.5 * float(AXIS[j1]) ** 2 + LOG_TOTAL))

    def tables(k, tab_ref, at):
        base, ratio0, ratio1, c = tile_start(par_ref, k, first)
        c_b = jnp.broadcast_to(c, (SIDE, TILE))
        log_rest = jnp.broadcast_to(jnp.log(1.0 - c), (SIDE, TILE))
        for j0 in range(HALF):
            u = base
            for j1 in range(SIDE):
                rows = pl.ds((j0 * SIDE + j1) * SIDE, SIDE)
                log_one = jnp.log(1.0 + u)
                tab_ref[rows, at : at + TILE] = (jnp.log(c_b + u) - log_one).astype(BF16)
                tab_ref[rows, at + TILE : at + 2 * TILE] = (log_rest - log_one).astype(BF16)
                u = u * ratio1
            base = base * ratio0

    def mark(k, mark_ref, at):
        codes = jnp.transpose(resp_ref[k].astype(F32))
        live = par_ref[5, pl.ds(k, 1), :]
        mark_ref[at : at + TILE, :] = jnp.where(codes == 2.0, live, 0.0).astype(BF16)
        mark_ref[at + TILE : at + 2 * TILE, :] = jnp.where(codes == 1.0, live, 0.0).astype(BF16)

    def gather(tab_ref, mark_ref):
        marks = mark_ref[...]
        for s in range(0, HERE, 4 * SLAB):
            w_ref[s : s + 4 * SLAB, :] += jnp.dot(tab_ref[s : s + 4 * SLAB, :], marks, preferred_element_type=F32)

    def fill(pair, tab_ref, mark_ref):
        for side in range(2):
            k = 2 * pair + side
            mark(k, mark_ref, 2 * TILE * side)
            tables(k, tab_ref, 2 * TILE * side)

    def both(step, carry):
        fill(2 * step + 1, tab_b, mark_b)
        gather(tab_a, mark_a)
        fill(2 * step + 2, tab_a, mark_a)
        gather(tab_b, mark_b)
        return carry

    fill(0, tab_a, mark_a)
    lax.fori_loop(0, KT // 4 - 1, both, 0)
    fill(KT // 2 - 1, tab_b, mark_b)
    gather(tab_a, mark_a)
    gather(tab_b, mark_b)

    top = jnp.full((SIDE, TILE), -jnp.inf, F32)
    for j in range(HALF * SIDE):
        top = jnp.maximum(top, w_ref[j * SIDE : (j + 1) * SIDE, :])
    top = jnp.max(top, axis=0, keepdims=True)
    total = jnp.zeros((SIDE, TILE), F32)
    mom0 = jnp.zeros((SIDE, TILE), F32)
    mom1 = jnp.zeros((SIDE, TILE), F32)
    for j0 in range(HALF):
        slab_sum = jnp.zeros((SIDE, TILE), F32)
        for j1 in range(SIDE):
            rows = pl.ds((j0 * SIDE + j1) * SIDE, SIDE)
            w = jnp.exp(w_ref[rows, :] - top)
            w_ref[rows, :] = w
            slab_sum = slab_sum + w
            mom1 = mom1 + float(AXIS[j1]) * w
        total = total + slab_sum
        mom0 = mom0 + (first + STEP * j0) * slab_sum
    st_ref[0:1, :] = top
    for j, part in enumerate((total, mom0, mom1, total * theta2)):
        st_ref[j + 1 : j + 2, :] = jnp.sum(part, axis=0, keepdims=True)
    st_ref[5:8, :] = jnp.zeros((3, TILE), F32)


def statistics_kernel(place_ref, got_ref, resp_ref, w_ref, mine_ref, other_ref, out_ref, par_ref, post_ref):
    first = first_theta0(place_ref)
    par_ref[...] = got_ref[...].astype(F32)
    mine, other = mine_ref[...], other_ref[...]
    top = jnp.maximum(mine[0:1], other[0:1])
    both = mine[1:5] * jnp.exp(mine[0:1] - top) + other[1:5] * jnp.exp(other[0:1] - top)
    log_norm = top + jnp.log(both[0:1])
    means = both[1:4] / both[0:1]
    scale = jnp.exp(mine[0:1] - log_norm)
    post_ref[...] = (w_ref[...] * scale).astype(BF16)
    for j in range(8):
        out_ref[j, KT : KT + 1, :] = log_norm
        out_ref[j, KT + 1 : KT + 4, :] = means
    theta2 = axis_column()
    zero = jnp.zeros((SIDE, TILE), F32)
    zero_h = jnp.zeros((HALF, TILE), F32)

    def tile(k):
        a0, a1, a2, d, c, live = (par_ref[j, pl.ds(k, 1), :] for j in range(6))
        codes = resp_ref[k]
        hit, any_answer = jnp.where(codes == 2, live, 0.0), jnp.where(codes > 0, live, 0.0)
        marks = jnp.concatenate([hit.astype(BF16), any_answer.astype(BF16)], axis=1)
        base = jnp.exp(a2 * theta2 + (a0 * first + a1 * float(AXIS[0]) + d))
        ratio0 = jnp.broadcast_to(jnp.exp(a0 * STEP), (SIDE, TILE))
        ratio1 = jnp.broadcast_to(jnp.exp(a1 * STEP), (SIDE, TILE))
        c_b = jnp.broadcast_to(c, (SIDE, TILE))
        g_all, g_0, g_run = zero, zero, zero_h
        f_all, f_0, f_1 = zero_h, zero_h, zero_h
        for j0 in range(HALF):
            counts = jnp.dot(post_ref[j0 * SLAB : (j0 + 1) * SLAB, :], marks, preferred_element_type=F32)
            theta0 = first + STEP * j0
            u = base
            g_slab, f_slab, infos = zero, zero_h, []
            for j1 in range(SIDE):
                hits = counts[j1 * SIDE : (j1 + 1) * SIDE, 0:TILE]
                mass = counts[j1 * SIDE : (j1 + 1) * SIDE, TILE : 2 * TILE]
                miss = 1.0 / (1.0 + u)
                share = u * (1.0 / (c_b + u))
                mass_sig = mass * (u * miss)
                info = mass_sig * (share * miss)
                g_slab = g_slab + (hits * share - mass_sig)
                g_run = g_run + (g_slab[:HALF] + g_slab[HALF:])
                infos.append(info)
                if j1 >= HALF:
                    info = info + infos[SIDE - 1 - j1]
                    info = info[:HALF] + info[HALF:]
                    f_slab = f_slab + info
                    f_1 = f_1 + float(AXIS[j1]) ** 2 * info
                u = u * ratio1
            g_all, f_all = g_all + g_slab, f_all + f_slab
            g_0, f_0 = g_0 + theta0 * g_slab, f_0 + (theta0 * theta0) * f_slab
            base = base * ratio0
        square = theta2[:HALF] * theta2[:HALF]
        g_sum = g_all[:HALF] + g_all[HALF:]
        g_1 = (float(AXIS[-1]) + STEP) * g_sum - STEP * g_run
        rest = 1.0 - c
        rows = (g_0, g_1, theta2 * g_all, g_sum, f_0, f_1, square * f_all, f_all)
        for j, part in enumerate(rows):
            summed = jnp.sum(part, axis=0, keepdims=True)
            out_ref[j, pl.ds(k, 1), :] = summed if j < 4 else summed * rest

    @pl.loop(0, KT // 4)
    def _(step):
        for side in range(4):
            tile(4 * step + side)


def spread_kernel(turn_ref, got_ref, out_ref):
    both = []
    for b in range(4):
        both.append(got_ref[2 * b] + got_ref[2 * b + 1])
    both.extend([jnp.zeros((4 * SLOTS, TILE), F32)])
    both = jnp.concatenate(both, axis=0)
    high = both.astype(BF16)
    low = (both - high.astype(F32)).astype(BF16)
    turn = turn_ref[...]
    total = jnp.dot(turn, high, preferred_element_type=F32) + jnp.dot(turn, low, preferred_element_type=F32)
    out_ref[...] = total.astype(BF16)


def gather_kernel(got_ref, out_ref):
    total = jnp.sum(got_ref[...].astype(F32), axis=0)
    out_ref[...] = jnp.broadcast_to(total[None], out_ref.shape)


def update_kernel(slopes_ref, icpt_ref, part_ref, got_ref, out_ref, marg_ref, mean_ref):
    for b in range(4):
        marg_ref[0:1, b * TILE : (b + 1) * TILE] = part_ref[2 * b, KT : KT + 1, :]
        mean_ref[:, b * TILE : (b + 1) * TILE] = part_ref[2 * b, KT + 1 : KT + 4, :]
    slopes = slopes_ref[...].astype(F32)
    icpt = icpt_ref[...].astype(F32)
    for p in range(4):
        step = got_ref[p] / (got_ref[p + 4] + 1.0)
        for j in range(step.shape[0]):
            span = slice(j * TILE, (j + 1) * TILE)
            now = slopes[p : p + 1, span] if p < 3 else icpt[j : j + 1]
            out_ref[p : p + 1, span] = now + step[j : j + 1]


def shape(dims, kind=F32):
    return jax.ShapeDtypeStruct(dims, kind)


def local(slopes, intercepts, guessing, responses, tile_items, tile_count):
    takers = lax.axis_size("takers")
    place = lax.axis_index("nodes").reshape(1)
    block = place >> 1
    own = slopes.shape[1]
    rows = own // TILE
    blocks = takers * rows
    icpt, guess = intercepts.reshape(rows, TILE), guessing.reshape(rows, TILE)
    offer = pl.pallas_call(
        offer_kernel,
        out_shape=shape((takers, rows, TILE), BF16),
        in_specs=[SMEM, HBM, HBM, HBM],
        out_specs=VMEM,
        scratch_shapes=[
            pltpu.VMEM((3, own), BF16),
            pltpu.VMEM((rows, TILE), BF16),
            pltpu.VMEM((rows, TILE), BF16),
            pltpu.SemaphoreType.DMA((3,)),
        ],
        compiler_params=params(60),
        name="offer",
    )(place, slopes, icpt, guess)
    pick, turn = pl.pallas_call(
        plan_kernel,
        out_shape=(shape((TILE, blocks), BF16), shape((blocks, TILE), BF16)),
        in_specs=[SMEM, SMEM],
        out_specs=(VMEM, VMEM),
        scratch_shapes=[pltpu.VMEM((TILE, blocks), F32)],
        compiler_params=params(6),
        name="plan",
    )(tile_count, tile_items)
    table = lax.all_to_all(offer, "takers", 0, 0).reshape(blocks, TILE)
    picked = pl.pallas_call(
        pick_kernel,
        out_shape=shape((8, SLOTS, TILE), BF16),
        in_specs=[SMEM, SMEM, VMEM, VMEM],
        out_specs=VMEM,
        compiler_params=params(4),
        name="pick",
    )(place, block, pick, table)
    got, block = lax.optimization_barrier((lax.all_to_all(picked, "nodes", 0, 0), block))
    answers = lax.dynamic_index_in_dim(responses, block[0], 0, keepdims=False)
    weights, state = pl.pallas_call(
        likelihood_kernel,
        out_shape=(shape((HERE, TILE)), shape((8, TILE))),
        in_specs=[SMEM, VMEM, VMEM],
        out_specs=(VMEM, VMEM),
        scratch_shapes=[
            pltpu.VMEM((8, SLOTS, TILE), F32),
            pltpu.VMEM((HERE, 4 * TILE), BF16),
            pltpu.VMEM((HERE, 4 * TILE), BF16),
            pltpu.VMEM((4 * TILE, TILE), BF16),
            pltpu.VMEM((4 * TILE, TILE), BF16),
        ],
        compiler_params=params(14),
        name="likelihood",
    )(place, got, answers)
    other = lax.ppermute(state, "nodes", [(i, i ^ 1) for i in range(8)])
    stats = pl.pallas_call(
        statistics_kernel,
        out_shape=shape((8, SLOTS, TILE)),
        in_specs=[SMEM, VMEM, VMEM, VMEM, VMEM, VMEM],
        out_specs=VMEM,
        scratch_shapes=[pltpu.VMEM((8, SLOTS, TILE), F32), pltpu.VMEM((HERE, TILE), BF16)],
        compiler_params=params(14),
        name="statistics",
    )(place, got, answers, weights, state, other)
    partial = lax.all_to_all(stats, "nodes", 0, 0)
    spread = pl.pallas_call(
        spread_kernel,
        out_shape=shape((blocks, TILE), BF16),
        in_specs=[VMEM, VMEM],
        out_specs=VMEM,
        compiler_params=params(4),
        name="spread",
    )(turn, partial)
    owned = lax.all_to_all(spread.reshape(takers, rows, TILE), "takers", 0, 0)
    summed = pl.pallas_call(
        gather_kernel,
        out_shape=shape((8, rows, TILE)),
        in_specs=[VMEM],
        out_specs=VMEM,
        compiler_params=params(4),
        name="gather",
    )(owned)
    new_params, marginal, means = pl.pallas_call(
        update_kernel,
        out_shape=(shape((4, own)), shape((1, 4 * TILE)), shape((3, 4 * TILE))),
        in_specs=[VMEM, VMEM, VMEM, VMEM],
        out_specs=(VMEM, VMEM, VMEM),
        compiler_params=params(4),
        name="update",
    )(slopes, icpt, partial, lax.all_to_all(summed, "nodes", 0, 0))
    return new_params, marginal.reshape(-1), means


def solution(mesh):
    in_specs = (
        P(None, "takers"),
        P("takers"),
        P("takers"),
        P("takers", None, None, None),
        P("takers", None),
        P("takers"),
    )
    out_specs = (P(None, "takers"), P("takers"), P(None, "takers"))
    return jax.shard_map(local, mesh=mesh, in_specs=in_specs, out_specs=out_specs, check_vma=False)
```

```python
import math

import jax
import jax.numpy as jnp
import numpy as np
from jax import lax
from jax.experimental import pallas as pl
from jax.experimental.pallas import tpu as pltpu
from jax.sharding import PartitionSpec as P

SIDE = 16
HALF = SIDE // 2
TILE = 128
KT = 12
SLOTS = 16
SLAB = SIDE * SIDE
HERE = HALF * SLAB
F32 = jnp.float32
BF16 = jnp.bfloat16
STEP = 6.0 / 15.0

AXIS = (np.float32(-3.0) + np.float32(6.0) * np.arange(SIDE, dtype=np.float32) / np.float32(15.0)).astype(np.float32)
LOG_TOTAL = 3.0 * math.log(float(np.sum(np.exp(-0.5 * AXIS.astype(np.float64) ** 2))))

VMEM = pl.BlockSpec(memory_space=pltpu.VMEM)
SMEM = pl.BlockSpec(memory_space=pltpu.SMEM)
HBM = pl.BlockSpec(memory_space=pltpu.HBM)


def params(mib):
    return pltpu.CompilerParams(vmem_limit_bytes=mib << 20)


def axis_column():
    index = lax.broadcasted_iota(jnp.int32, (SIDE, TILE), 0)
    index = jnp.where(index < HALF, index, SIDE + HALF - 1 - index).astype(F32)
    return -3.0 + 6.0 * index / 15.0


def first_theta0(place_ref):
    return -3.0 + STEP * HALF * (place_ref[0] & 1).astype(F32)


def tile_start(par_ref, k, first):
    a0, a1, a2, d, c = (par_ref[j, pl.ds(k, 1), :] for j in range(5))
    base = jnp.exp(a2 * axis_column() + (a0 * first + a1 * float(AXIS[0]) + d))
    ratio0 = jnp.broadcast_to(jnp.exp(a0 * STEP), (SIDE, TILE))
    ratio1 = jnp.broadcast_to(jnp.exp(a1 * STEP), (SIDE, TILE))
    return base, ratio0, ratio1, c


def offer_kernel(place_ref, slopes_hbm, icpt_hbm, guess_hbm, out_ref, slopes_ref, icpt_ref, guess_ref, sem_ref):
    copies = [
        pltpu.make_async_copy(slopes_hbm, slopes_ref, sem_ref.at[0]),
        pltpu.make_async_copy(icpt_hbm, icpt_ref, sem_ref.at[1]),
        pltpu.make_async_copy(guess_hbm, guess_ref, sem_ref.at[2]),
    ]
    for copy in copies:
        copy.start()
    for copy in copies:
        copy.wait()
    place = place_ref[0]
    slopes = slopes_ref[...].astype(F32)
    row = jnp.where(place == 0, slopes[0:1], jnp.where(place == 1, slopes[1:2], slopes[2:3]))
    rows = jnp.concatenate([row[:, j * TILE : (j + 1) * TILE] for j in range(row.shape[1] // TILE)], axis=0)
    rows = jnp.where(place == 3, icpt_ref[...].astype(F32), rows)
    rows = jnp.where(place >= 4, guess_ref[...].astype(F32), rows)
    out_ref[...] = jnp.broadcast_to(rows.astype(BF16)[None], out_ref.shape)


def plan_kernel(count_ref, items_ref, pick_ref, turn_ref, wide_ref):
    wide_ref[...] = jnp.zeros(wide_ref.shape, F32)
    blocks = wide_ref.shape[1]
    block_of = lax.broadcasted_iota(jnp.int32, (1, blocks), 1)
    for b in range(4):
        for k in range(KT):
            at = b * SLOTS + k
            wide_ref[at : at + 1, :] = (block_of == items_ref[b, k]).astype(F32)
            at += 4 * SLOTS
            wide_ref[at : at + 1, 0:TILE] = jnp.full((1, TILE), k < count_ref[b]).astype(F32)
    pick_ref[...] = wide_ref[...].astype(BF16)
    for j in range(blocks // TILE):
        turn_ref[j * TILE : (j + 1) * TILE, :] = jnp.transpose(wide_ref[:, j * TILE : (j + 1) * TILE]).astype(BF16)


def pick_kernel(place_ref, block_ref, pick_ref, table_ref, out_ref):
    rows = jnp.dot(pick_ref[0 : 4 * SLOTS, :], table_ref[...], preferred_element_type=F32)
    live = pick_ref[4 * SLOTS : 8 * SLOTS, 0:TILE].astype(F32)
    rows = jnp.where(place_ref[0] == 5, live, rows).astype(BF16)
    for b in range(4):
        out_ref[2 * b] = rows[b * SLOTS : (b + 1) * SLOTS]
        out_ref[2 * b + 1] = rows[b * SLOTS : (b + 1) * SLOTS]


def likelihood_kernel(place_ref, got_ref, resp_ref, w_ref, st_ref, par_ref, tab_a, tab_b, mark_a, mark_b):
    first = first_theta0(place_ref)
    par_ref[...] = got_ref[...].astype(F32)
    theta2 = axis_column()
    half_square = -0.5 * (theta2 * theta2)
    for j0 in range(HALF):
        theta0 = first + STEP * j0
        for j1 in range(SIDE):
            rows = pl.ds((j0 * SIDE + j1) * SIDE, SIDE)
            w_ref[rows, :] = half_square - (0.5 * (theta0 * theta0) + (0.5 * float(AXIS[j1]) ** 2 + LOG_TOTAL))

    def tables(k, tab_ref, at):
        base, ratio0, ratio1, c = tile_start(par_ref, k, first)
        c_b = jnp.broadcast_to(c, (SIDE, TILE))
        log_rest = jnp.broadcast_to(jnp.log(1.0 - c), (SIDE, TILE))
        for j0 in range(HALF):
            u = base
            for j1 in range(SIDE):
                rows = pl.ds((j0 * SIDE + j1) * SIDE, SIDE)
                log_one = jnp.log(1.0 + u)
                tab_ref[rows, at : at + TILE] = (jnp.log(c_b + u) - log_one).astype(BF16)
                tab_ref[rows, at + TILE : at + 2 * TILE] = (log_rest - log_one).astype(BF16)
                u = u * ratio1
            base = base * ratio0

    def mark(k, mark_ref, at):
        codes = jnp.transpose(resp_ref[k].astype(F32))
        live = par_ref[5, pl.ds(k, 1), :]
        mark_ref[at : at + TILE, :] = jnp.where(codes == 2.0, live, 0.0).astype(BF16)
        mark_ref[at + TILE : at + 2 * TILE, :] = jnp.where(codes == 1.0, live, 0.0).astype(BF16)

    def gather(tab_ref, mark_ref):
        marks = mark_ref[...]
        for s in range(0, HERE, 4 * SLAB):
            w_ref[s : s + 4 * SLAB, :] += jnp.dot(tab_ref[s : s + 4 * SLAB, :], marks, preferred_element_type=F32)

    def fill(pair, tab_ref, mark_ref):
        for side in range(2):
            k = 2 * pair + side
            mark(k, mark_ref, 2 * TILE * side)
            tables(k, tab_ref, 2 * TILE * side)

    def both(step, carry):
        fill(2 * step + 1, tab_b, mark_b)
        gather(tab_a, mark_a)
        fill(2 * step + 2, tab_a, mark_a)
        gather(tab_b, mark_b)
        return carry

    fill(0, tab_a, mark_a)
    lax.fori_loop(0, KT // 4 - 1, both, 0)
    fill(KT // 2 - 1, tab_b, mark_b)
    gather(tab_a, mark_a)
    gather(tab_b, mark_b)

    top = jnp.full((SIDE, TILE), -jnp.inf, F32)
    for j in range(HALF * SIDE):
        top = jnp.maximum(top, w_ref[j * SIDE : (j + 1) * SIDE, :])
    top = jnp.max(top, axis=0, keepdims=True)
    total = jnp.zeros((SIDE, TILE), F32)
    mom0 = jnp.zeros((SIDE, TILE), F32)
    mom1 = jnp.zeros((SIDE, TILE), F32)
    for j0 in range(HALF):
        slab_sum = jnp.zeros((SIDE, TILE), F32)
        for j1 in range(SIDE):
            rows = pl.ds((j0 * SIDE + j1) * SIDE, SIDE)
            w = jnp.exp(w_ref[rows, :] - top)
            w_ref[rows, :] = w
            slab_sum = slab_sum + w
            mom1 = mom1 + float(AXIS[j1]) * w
        total = total + slab_sum
        mom0 = mom0 + (first + STEP * j0) * slab_sum
    st_ref[0:1, :] = top
    for j, part in enumerate((total, mom0, mom1, total * theta2)):
        st_ref[j + 1 : j + 2, :] = jnp.sum(part, axis=0, keepdims=True)
    st_ref[5:8, :] = jnp.zeros((3, TILE), F32)


def marks_kernel(got_ref, resp_ref, out_ref):
    live = got_ref[5].astype(F32)
    for k in range(KT):
        codes, used = resp_ref[k], live[k : k + 1]
        out_ref[k, :, 0:TILE] = jnp.where(codes == 2, used, 0.0).astype(BF16)
        out_ref[k, :, TILE : 2 * TILE] = jnp.where(codes > 0, used, 0.0).astype(BF16)


def statistics_kernel(place_ref, got_ref, marks_ref, w_ref, mine_ref, other_ref, out_ref, par_ref, post_ref):
    first = first_theta0(place_ref)
    par_ref[...] = got_ref[...].astype(F32)
    mine, other = mine_ref[...], other_ref[...]
    top = jnp.maximum(mine[0:1], other[0:1])
    both = mine[1:5] * jnp.exp(mine[0:1] - top) + other[1:5] * jnp.exp(other[0:1] - top)
    log_norm = top + jnp.log(both[0:1])
    means = both[1:4] / both[0:1]
    scale = jnp.exp(mine[0:1] - log_norm)
    post_ref[...] = (w_ref[...] * scale).astype(BF16)
    for j in range(8):
        out_ref[j, KT : KT + 1, :] = log_norm
        out_ref[j, KT + 1 : KT + 4, :] = means
    theta2 = axis_column()
    zero = jnp.zeros((SIDE, TILE), F32)
    zero_h = jnp.zeros((HALF, TILE), F32)

    def tile(k):
        a0, a1, a2, d, c = (par_ref[j, pl.ds(k, 1), :] for j in range(5))
        marks = marks_ref[k]
        base = jnp.exp(-(a2 * theta2 + (a0 * first + a1 * float(AXIS[0]) + d)))
        ratio0 = jnp.broadcast_to(jnp.exp(a0 * -STEP), (SIDE, TILE))
        ratio1 = jnp.broadcast_to(jnp.exp(a1 * -STEP), (SIDE, TILE))
        c_b = jnp.broadcast_to(c, (SIDE, TILE))
        g_all, g_0, g_run = zero, zero, zero_h
        f_all, f_0, f_1 = zero_h, zero_h, zero_h
        for j0 in range(HALF):
            counts = jnp.dot(post_ref[j0 * SLAB : (j0 + 1) * SLAB, :], marks, preferred_element_type=F32)
            theta0 = first + STEP * j0
            e, ce = base, base * c_b
            g_slab, f_slab, infos = zero, zero_h, []
            for j1 in range(SIDE):
                hits = counts[j1 * SIDE : (j1 + 1) * SIDE, 0:TILE]
                mass = counts[j1 * SIDE : (j1 + 1) * SIDE, TILE : 2 * TILE]
                sig = 1.0 / (1.0 + e)
                share = 1.0 / (1.0 + ce)
                miss = e * sig
                mass_sig = mass * sig
                info = mass_sig * (share * miss)
                g_slab = g_slab + (hits * share - mass_sig)
                g_run = g_run + (g_slab[:HALF] + g_slab[HALF:])
                infos.append(info)
                if j1 >= HALF:
                    info = info + infos[SIDE - 1 - j1]
                    info = info[:HALF] + info[HALF:]
                    f_slab = f_slab + info
                    f_1 = f_1 + float(AXIS[j1]) ** 2 * info
                e, ce = e * ratio1, ce * ratio1
            g_all, f_all = g_all + g_slab, f_all + f_slab
            g_0, f_0 = g_0 + theta0 * g_slab, f_0 + (theta0 * theta0) * f_slab
            base = base * ratio0
        square = theta2[:HALF] * theta2[:HALF]
        g_sum = g_all[:HALF] + g_all[HALF:]
        g_1 = (float(AXIS[-1]) + STEP) * g_sum - STEP * g_run
        rest = 1.0 - c
        rows = (g_0, g_1, theta2 * g_all, g_sum, f_0, f_1, square * f_all, f_all)
        for j, part in enumerate(rows):
            summed = jnp.sum(part, axis=0, keepdims=True)
            out_ref[j, pl.ds(k, 1), :] = summed if j < 4 else summed * rest

    @pl.loop(0, KT // 6)
    def _(step):
        for side in range(6):
            tile(6 * step + side)


def spread_kernel(turn_ref, got_ref, out_ref):
    both = []
    for b in range(4):
        both.append(got_ref[2 * b] + got_ref[2 * b + 1])
    both.extend([jnp.zeros((4 * SLOTS, TILE), F32)])
    both = jnp.concatenate(both, axis=0)
    high = both.astype(BF16)
    low = (both - high.astype(F32)).astype(BF16)
    turn = turn_ref[...]
    total = jnp.dot(turn, high, preferred_element_type=F32) + jnp.dot(turn, low, preferred_element_type=F32)
    out_ref[...] = total.astype(BF16)


def gather_kernel(got_ref, out_ref):
    total = jnp.sum(got_ref[...].astype(F32), axis=0)
    out_ref[...] = jnp.broadcast_to(total[None], out_ref.shape)


def update_kernel(slopes_ref, icpt_ref, part_ref, got_ref, out_ref, marg_ref, mean_ref):
    for b in range(4):
        marg_ref[0:1, b * TILE : (b + 1) * TILE] = part_ref[2 * b, KT : KT + 1, :]
        mean_ref[:, b * TILE : (b + 1) * TILE] = part_ref[2 * b, KT + 1 : KT + 4, :]
    slopes = slopes_ref[...].astype(F32)
    icpt = icpt_ref[...].astype(F32)
    for p in range(4):
        step = got_ref[p] / (got_ref[p + 4] + 1.0)
        for j in range(step.shape[0]):
            span = slice(j * TILE, (j + 1) * TILE)
            now = slopes[p : p + 1, span] if p < 3 else icpt[j : j + 1]
            out_ref[p : p + 1, span] = now + step[j : j + 1]


def shape(dims, kind=F32):
    return jax.ShapeDtypeStruct(dims, kind)


def local(slopes, intercepts, guessing, responses, tile_items, tile_count):
    takers = lax.axis_size("takers")
    place = lax.axis_index("nodes").reshape(1)
    block = place >> 1
    own = slopes.shape[1]
    rows = own // TILE
    blocks = takers * rows
    icpt, guess = intercepts.reshape(rows, TILE), guessing.reshape(rows, TILE)
    offer = pl.pallas_call(
        offer_kernel,
        out_shape=shape((takers, rows, TILE), BF16),
        in_specs=[SMEM, HBM, HBM, HBM],
        out_specs=VMEM,
        scratch_shapes=[
            pltpu.VMEM((3, own), BF16),
            pltpu.VMEM((rows, TILE), BF16),
            pltpu.VMEM((rows, TILE), BF16),
            pltpu.SemaphoreType.DMA((3,)),
        ],
        compiler_params=params(60),
        name="offer",
    )(place, slopes, icpt, guess)
    pick, turn = pl.pallas_call(
        plan_kernel,
        out_shape=(shape((TILE, blocks), BF16), shape((blocks, TILE), BF16)),
        in_specs=[SMEM, SMEM],
        out_specs=(VMEM, VMEM),
        scratch_shapes=[pltpu.VMEM((TILE, blocks), F32)],
        compiler_params=params(6),
        name="plan",
    )(tile_count, tile_items)
    table = lax.all_to_all(offer, "takers", 0, 0).reshape(blocks, TILE)
    picked = pl.pallas_call(
        pick_kernel,
        out_shape=shape((8, SLOTS, TILE), BF16),
        in_specs=[SMEM, SMEM, VMEM, VMEM],
        out_specs=VMEM,
        compiler_params=params(4),
        name="pick",
    )(place, block, pick, table)
    got, block = lax.optimization_barrier((lax.all_to_all(picked, "nodes", 0, 0), block))
    answers = lax.dynamic_index_in_dim(responses, block[0], 0, keepdims=False)
    weights, state = pl.pallas_call(
        likelihood_kernel,
        out_shape=(shape((HERE, TILE)), shape((8, TILE))),
        in_specs=[SMEM, VMEM, VMEM],
        out_specs=(VMEM, VMEM),
        scratch_shapes=[
            pltpu.VMEM((8, SLOTS, TILE), F32),
            pltpu.VMEM((HERE, 4 * TILE), BF16),
            pltpu.VMEM((HERE, 4 * TILE), BF16),
            pltpu.VMEM((4 * TILE, TILE), BF16),
            pltpu.VMEM((4 * TILE, TILE), BF16),
        ],
        compiler_params=params(14),
        name="likelihood",
    )(place, got, answers)
    state, answers = lax.optimization_barrier((state, answers))
    other = lax.ppermute(state, "nodes", [(i, i ^ 1) for i in range(8)])
    marks = pl.pallas_call(
        marks_kernel,
        out_shape=shape((KT, TILE, 2 * TILE), BF16),
        in_specs=[VMEM, VMEM],
        out_specs=VMEM,
        compiler_params=params(6),
        name="marks",
    )(got, answers)
    stats = pl.pallas_call(
        statistics_kernel,
        out_shape=shape((8, SLOTS, TILE)),
        in_specs=[SMEM, VMEM, VMEM, VMEM, VMEM, VMEM],
        out_specs=VMEM,
        scratch_shapes=[pltpu.VMEM((8, SLOTS, TILE), F32), pltpu.VMEM((HERE, TILE), BF16)],
        compiler_params=params(14),
        name="statistics",
    )(place, got, marks, weights, state, other)
    partial = lax.all_to_all(stats, "nodes", 0, 0)
    spread = pl.pallas_call(
        spread_kernel,
        out_shape=shape((blocks, TILE), BF16),
        in_specs=[VMEM, VMEM],
        out_specs=VMEM,
        compiler_params=params(4),
        name="spread",
    )(turn, partial)
    owned = lax.all_to_all(spread.reshape(takers, rows, TILE), "takers", 0, 0)
    summed = pl.pallas_call(
        gather_kernel,
        out_shape=shape((8, rows, TILE)),
        in_specs=[VMEM],
        out_specs=VMEM,
        compiler_params=params(4),
        name="gather",
    )(owned)
    new_params, marginal, means = pl.pallas_call(
        update_kernel,
        out_shape=(shape((4, own)), shape((1, 4 * TILE)), shape((3, 4 * TILE))),
        in_specs=[VMEM, VMEM, VMEM, VMEM],
        out_specs=(VMEM, VMEM, VMEM),
        compiler_params=params(4),
        name="update",
    )(slopes, icpt, partial, lax.all_to_all(summed, "nodes", 0, 0))
    return new_params, marginal.reshape(-1), means


def solution(mesh):
    in_specs = (
        P(None, "takers"),
        P("takers"),
        P("takers"),
        P("takers", None, None, None),
        P("takers", None),
        P("takers"),
    )
    out_specs = (P(None, "takers"), P("takers"), P(None, "takers"))
    return jax.shard_map(local, mesh=mesh, in_specs=in_specs, out_specs=out_specs, check_vma=False)
```
